256 devices in a mesh: br: 64 (over z, y_hi, x), bus: 4 (over y_lo, core).
Axes of the slice: x: 4, y: 4 (y_hi: 2, y_lo: 2; y = y_hi * 2 + y_lo), z: 8, core: 2. Of those that a mesh axis runs over, the one named last changes fastest.
Arguments:
- net_load: bfloat16 [128, 60416], P('br', 'bus'), may hold values from -6 to 6
- release: float32 [128, 1024], P('br'), may hold values from 0 to 2
- plant_bus: int32 [1024], replicated, may hold values from 0 to 60415
- efficiency: float32 [1024], replicated, may hold values from 0.5 to 2
- ptdf: bfloat16 [8192, 60416], P('br', 'bus'), may hold values from -0.0234375 to 0.0234375
- branch_class: int32 [8192], P('br'), may hold values from 0 to 15
- class_limit: float32 [16], replicated, may hold values from 0.4 to 3
- class_price: float32 [16], replicated, may hold values from 0.5 to 5
Outputs:
- grad_bus: float32 [128, 60416], P('br', 'bus')
- grad_release: float32 [128, 1024], P('br')
The draws below stay inside these ranges and needn't reach their ends.
All inputs are finite; a program needn't handle non-finite values.
Results may differ from the reference program's by a relative error of at most 0.0031.
Values may be sent and summed in bfloat16 or wider, within the bound.
A program may use at most 64 MiB of HBM per device.

```python
import math
import jax
import jax.numpy as jnp
from jax import lax

BUSES = 60416
BRANCHES = 8192
SCEN = 128
PLANTS = 1024
CLASSES = 16


def with_ends(array, stream_key, least, high):
    shape = array.shape
    index_at = [jax.random.randint(jax.random.fold_in(stream_key, axis), (), 0, shape[axis]) for axis in range(len(shape))]
    array = array.at[tuple(index_at)].set(least)
    longest = shape.index(max(shape))
    index_at[longest] = (index_at[longest] + 1) % shape[longest]
    return array.at[tuple(index_at)].set(high)


def shard_levels(rng, shape, split, smallest, high):
    def one(position, parts):
        draws = jax.random.uniform(jax.random.fold_in(jax.random.fold_in(rng, 6), position), (parts,), jnp.float32, smallest / len(split), high / len(split))
        return jnp.repeat(jnp.exp(draws), shape[position] // parts).reshape((-1,) + (1,) * (len(shape) - position - 1))

    level = one(*split[0])
    for cut in split[1:]:
        level = level * one(*cut)
    return level


def gaussian(stream_key, shape, width, bound, cuts=(), dtype=jnp.bfloat16):
    factor_of = shard_levels(stream_key, shape, cuts, -0.22, 0.18) if cuts else 1.0
    array = jax.random.normal(stream_key, shape, jnp.float32) * width * factor_of
    return jnp.minimum(jnp.maximum(array, -bound), bound).astype(dtype)


def setup_inputs(seed: int = 0) -> dict:
    seeds = jax.random.split(jax.random.key(seed), 9)
    net_load = gaussian(seeds[0], (SCEN, BUSES), 1.0, 6.0, ((0, 64), (1, 4)))
    release = jnp.clip(2.0 * jax.random.uniform(seeds[1], (SCEN, PLANTS), jnp.float32) ** shard_levels(seeds[1], (SCEN, PLANTS), ((0, 64),), -0.2, 0.2), 0.0, 2.0)
    plant_bus = with_ends(jax.random.randint(seeds[2], (PLANTS,), 0, BUSES), jax.random.fold_in(seeds[2], 1), 0, BUSES - 1).astype(jnp.int32)
    efficiency = jnp.clip(jnp.exp(jax.random.uniform(seeds[3], (PLANTS,), jnp.float32, math.log(0.5), math.log(2.0))), 0.5, 2.0)
    ptdf = gaussian(seeds[4], (BRANCHES, BUSES), BUSES ** -0.5, 0.0234375, ((0, 64), (1, 4)))
    branch_class = with_ends(jax.random.randint(seeds[5], (BRANCHES,), 0, CLASSES), jax.random.fold_in(seeds[5], 1), 0, CLASSES - 1).astype(jnp.int32)
    class_limit = jnp.clip(jnp.exp(jax.random.uniform(seeds[6], (CLASSES,), jnp.float32, math.log(0.4), math.log(3.0))), 0.4, 3.0)
    class_price = jnp.clip(jnp.exp(jax.random.uniform(seeds[7], (CLASSES,), jnp.float32, math.log(0.5), math.log(5.0))), 0.5, 5.0)
    return dict(net_load=net_load, release=release, plant_bus=plant_bus, efficiency=efficiency, ptdf=ptdf, branch_class=branch_class, class_limit=class_limit, class_price=class_price)


SMOOTH = 0.25


def reference(net_load, release, plant_bus, efficiency, ptdf, branch_class, class_limit, class_price):
    inject = net_load.astype(jnp.float32).at[:, plant_bus].add(release * efficiency[None, :]).astype(jnp.bfloat16)
    flows = lax.dot_general(inject, ptdf, (((1,), (1,)), ((), ())), preferred_element_type=jnp.float32)
    limit = class_limit[branch_class][None, :]
    price = class_price[branch_class][None, :]
    grad_flow = (price * (jax.nn.sigmoid((flows - limit) / SMOOTH) - jax.nn.sigmoid((-flows - limit) / SMOOTH))).astype(jnp.bfloat16)
    grad_bus = jnp.dot(grad_flow, ptdf, preferred_element_type=jnp.float32)
    grad_release = grad_bus[:, plant_bus] * efficiency[None, :]
    return grad_bus, grad_release
```

```python
import functools

import jax
import jax.numpy as jnp
from jax import lax
from jax.experimental import pallas as pl
from jax.experimental.pallas import tpu as pltpu
from jax.sharding import PartitionSpec as P

SMOOTH = 0.25
LANES = 128
NX, NY, NZ = 4, 2, 8
MESH = pl.DeviceIdType.MESH
NT = (((1,), (1,)), ((), ()))
TN = (((0,), (0,)), ((), ()))
NN = (((1,), (0,)), ((), ()))


def mm(a, b, dims):
    return lax.dot_general(a, b, dims, preferred_element_type=jnp.float32)


def split3(v):
    one = v.astype(jnp.bfloat16)
    rest = v - one.astype(jnp.float32)
    two = rest.astype(jnp.bfloat16)
    three = (rest - two.astype(jnp.float32)).astype(jnp.bfloat16)
    return one, two, three


def kernel(
    sizes,
    net_ref, rel_ref, plant_ref, eff_ref, ptdf_ref, cls_ref, lim_ref, price_ref,
    gbus_ref, grel_ref,
    inj, acc, px, py, recv_in, xall, fpart, frecv, ftot, gx, gy, gpart, ring, sbuf, srecv, rows, prel,
    s_p, r_p, l_p, s_i, r_i, l_i, s_z, r_z, s_f, r_f, s_b, r_b, s_g, r_g, s_r, r_r, s_s, r_s, s_o, r_o,
):
    tiles, tx, ty, nbus, plants, classes = sizes
    wx, wy = tx * LANES, ty * LANES
    base_y = NX * wx
    width = wx + wy
    c0 = (width // LANES) // 2 * LANES
    chunks = ((0, c0), (c0, width - c0))
    br, bus = lax.axis_index("br"), lax.axis_index("bus")
    z, y, x = br // (NX * NY), (br // NX) % NY, br % NX
    me = y * NX + x

    def at(z_, y_, x_):
        return ((z_ * NY + y_) * NX + x_, bus)

    xy_offsets = [(dy, dx) for dy in range(NY) for dx in range(NX) if (dy, dx) != (0, 0)]

    def xy(dy, dx):
        return (y + dy) % NY, (x + dx) % NX

    zup, zdn = (z + 1) % NZ, (z + NZ - 1) % NZ
    partners = [at(z, *xy(dy, dx)) for dy, dx in xy_offsets]
    partners += [at(zup, y, x), at(zdn, y, x)]
    partners += [(br, (bus + d) % nbus) for d in range(1, nbus)]

    barrier = pltpu.get_barrier_semaphore()
    for p in partners:
        pl.semaphore_signal(barrier, inc=1, device_id=p, device_id_type=MESH)

    sends = []

    def send(src, dst, ss, rs, dev):
        c = pltpu.make_async_remote_copy(
            src_ref=src, dst_ref=dst, send_sem=ss, recv_sem=rs, device_id=dev, device_id_type=MESH
        )
        c.start()
        sends.append(c)
        return c

    def window_x(ref, q):
        return ref.at[:, pl.ds(pl.multiple_of(q * wx, LANES), wx)]

    def window_y(ref, q):
        return ref.at[:, pl.ds(pl.multiple_of(base_y + q * wy, LANES), wy)]

    own_px = pltpu.make_async_copy(window_x(ptdf_ref, x), px.at[x], l_p.at[0])
    own_py = pltpu.make_async_copy(window_y(ptdf_ref, y), py.at[y], l_p.at[1])
    own_px.start()
    own_py.start()
    pl.semaphore_wait(barrier, len(partners))

    col = plant_ref[...] - bus * (tiles * LANES)
    hi = col >> 7
    lo = col & 127
    row_id = lax.broadcasted_iota(jnp.int32, (2 * tiles, plants), 0)
    lo_id = lax.broadcasted_iota(jnp.int32, (LANES, plants), 0)
    lo_hot = (lo_id == lo).astype(jnp.float32).astype(jnp.bfloat16)
    eff = eff_ref[...]
    weight = rel_ref[...] * eff
    here = (row_id >> 1) == hi
    odd = (row_id & 1) == 1
    total = None
    for part in split3(weight):
        part = part.astype(jnp.float32)
        placed = jnp.where(here, jnp.where(odd, part[1:2, :], part[0:1, :]), 0.0)
        term = mm(placed.astype(jnp.bfloat16), lo_hot, NT)
        total = term if total is None else total + term
    acc[...] = total
    for h in range(tiles):
        cols = slice(h * LANES, (h + 1) * LANES)
        inj[:, cols] = (acc[2 * h : 2 * h + 2, :] + net_ref[:, cols].astype(jnp.float32)).astype(jnp.bfloat16)

    arrivals = []
    for k, (dy, dx) in enumerate(xy_offsets):
        y_, x_ = xy(dy, dx)
        dev = at(z, y_, x_)
        arrivals.append(send(window_x(inj, x_), recv_in.at[me, :, pl.ds(0, wx)], s_i.at[2 * k], r_i.at[2 * k], dev))
        arrivals.append(send(window_y(inj, y_), recv_in.at[me, :, pl.ds(wx, wy)], s_i.at[2 * k + 1], r_i.at[2 * k + 1], dev))
    own_ix = pltpu.make_async_copy(window_x(inj, x), recv_in.at[me, :, pl.ds(0, wx)], l_i.at[0])
    own_iy = pltpu.make_async_copy(window_y(inj, y), recv_in.at[me, :, pl.ds(wx, wy)], l_i.at[1])
    own_ix.start()
    own_iy.start()

    factor = []
    for k in range(1, NX):
        x_ = (x + k) % NX
        factor.append(send(window_x(ptdf_ref, x_), px.at[x], s_p.at[k - 1], r_p.at[k - 1], at(z, y, x_)))
    y_ = (y + 1) % NY
    factor.append(send(window_y(ptdf_ref, y_), py.at[y], s_p.at[NX - 1], r_p.at[NX - 1], at(z, y_, x)))

    cls = cls_ref[...]
    limit = jnp.zeros(cls.shape, jnp.float32)
    price = jnp.zeros(cls.shape, jnp.float32)
    for k in range(classes):
        limit = jnp.where(cls == k, lim_ref[k], limit)
        price = jnp.where(cls == k, price_ref[k], price)

    own_ix.wait()
    own_iy.wait()
    for c in arrivals:
        c.wait_recv()
    for i in range(NX * NY):
        xall[z, 2 * i : 2 * i + 2, :] = recv_in[i]

    def ring_gather(step, d, c):
        start, size = chunks[c]
        n = (z + NZ - (step - 1)) % NZ if d == 0 else (z + (step - 1)) % NZ
        block = xall.at[n, :, pl.ds(start, size)]
        return send(block, block, s_z.at[d, step - 1, c], r_z.at[d, step - 1, c], at(zup if d == 0 else zdn, y, x))

    flight = {}
    for step in range(1, NZ // 2 + 1):
        for c in range(2):
            for d in range(2):
                if step == NZ // 2 and c != d:
                    continue
                if step > 1:
                    flight[step - 1, d, c].wait_recv()
                flight[step, d, c] = ring_gather(step, d, c)
    half = NZ // 2
    flight[half - 1, 0, 1].wait_recv()
    flight[half - 1, 1, 0].wait_recv()
    for d in range(2):
        flight[half, d, d].wait_recv()

    own_px.wait()
    own_py.wait()
    for c in factor:
        c.wait_recv()
    scen = NZ * 2 * NX * NY
    lhs_x = xall[:, :, 0:wx].reshape(scen, wx)
    for q in range(NX):
        fpart[q] = mm(lhs_x, px[q], NT)
    lhs_y = xall[:, :, wx:width].reshape(scen, wy)
    for q in range(NY):
        fpart[NX + q] = mm(lhs_y, py[q], NT)

    back = []
    for k in range(1, NX):
        x_ = (x + k) % NX
        back.append(send(fpart.at[x_], frecv.at[k - 1], s_f.at[k - 1], r_f.at[k - 1], at(z, y, x_)))
    back.append(send(fpart.at[NX + y_], frecv.at[NX - 1], s_f.at[NX - 1], r_f.at[NX - 1], at(z, y_, x)))
    own = fpart[x] + fpart[NX + y]
    for k, c in enumerate(back):
        c.wait_recv()
        own = own + frecv[k]
    ftot[bus] = own
    over = []
    for d in range(1, nbus):
        over.append(send(ftot.at[bus], ftot.at[bus], s_b.at[d - 1], r_b.at[d - 1], (br, (bus + d) % nbus)))
    for c in over:
        c.wait_recv()
    flows = ftot[0]
    for b in range(1, nbus):
        flows = flows + ftot[b]
    upper = jax.nn.sigmoid((flows - limit) / SMOOTH)
    lower = jax.nn.sigmoid((-flows - limit) / SMOOTH)
    grad_flow = (price * (upper - lower)).astype(jnp.bfloat16)
    gx[x] = grad_flow
    gy[y] = grad_flow
    given = []
    for k in range(1, NX):
        x_ = (x + k) % NX
        given.append(send(gx.at[x], gx.at[x], s_g.at[k - 1], r_g.at[k - 1], at(z, y, x_)))
    given.append(send(gy.at[y], gy.at[y], s_g.at[NX - 1], r_g.at[NX - 1], at(z, y_, x)))
    for c in given:
        c.wait_recv()

    grad = mm(gx[0], px[0], NN)
    for q in range(1, NX):
        grad = grad + mm(gx[q], px[q], NN)
    gpart[:, :, 0:wx] = grad.reshape(NZ, scen // NZ, wx)
    grad = mm(gy[0], py[0], NN)
    for q in range(1, NY):
        grad = grad + mm(gy[q], py[q], NN)
    gpart[:, :, wx:width] = grad.reshape(NZ, scen // NZ, wy)

    down = {}
    for step in range(1, half + 1):
        for c in range(2):
            start, size = chunks[c]
            for d in range(2):
                if step == 1 and c != d:
                    continue
                away = half + 1 - step
                target = (z + away) % NZ if d == 0 else (z + NZ - away) % NZ
                value = gpart[target, :, start : start + size]
                if (step - 1, d, c) in down:
                    down[step - 1, d, c].wait_recv()
                    value = value + ring[1, d, step - 2, :, start : start + size].astype(jnp.float32)
                ring[0, d, step - 1, :, start : start + size] = value.astype(jnp.bfloat16)
                down[step, d, c] = send(
                    ring.at[0, d, step - 1, :, pl.ds(start, size)],
                    ring.at[1, d, step - 1, :, pl.ds(start, size)],
                    s_r.at[d, step - 1, c], r_r.at[d, step - 1, c],
                    at(zup if d == 0 else zdn, y, x),
                )
    for c in range(2):
        start, size = chunks[c]
        value = gpart[z, :, start : start + size]
        for d in range(2):
            down[half, d, c].wait_recv()
            value = value + ring[1, d, half - 1, :, start : start + size].astype(jnp.float32)
        for i in range(NX * NY):
            sbuf[i, :, start : start + size] = value[2 * i : 2 * i + 2, :]
    last = []
    for k, (dy, dx) in enumerate(xy_offsets):
        y2, x2 = xy(dy, dx)
        last.append(send(sbuf.at[y2 * NX + x2], srecv.at[me], s_s.at[k], r_s.at[k], at(z, y2, x2)))
    srecv[me] = sbuf[me]
    for c in last:
        c.wait_recv()
    for q in range(NX):
        part = srecv[q, :, 0:wx]
        for j in range(1, NY):
            part = part + srecv[j * NX + q, :, 0:wx]
        gbus_ref[:, q * wx : (q + 1) * wx] = part
    for q in range(NY):
        part = srecv[q * NX, :, wx:width]
        for j in range(1, NX):
            part = part + srecv[q * NX + j, :, wx:width]
        gbus_ref[:, base_y + q * wy : base_y + (q + 1) * wy] = part

    for h in range(tiles):
        rows[2 * h : 2 * h + 2, :] = gbus_ref[:, h * LANES : (h + 1) * LANES]
    parts = split3(rows[...])
    lo_mask = lo_id == lo
    for s in range(2):
        hot = jnp.where(here & (odd == (s == 1)), 1.0, 0.0).astype(jnp.bfloat16)
        picked = mm(parts[0], hot, TN) + mm(parts[1], hot, TN) + mm(parts[2], hot, TN)
        picked = jnp.sum(jnp.where(lo_mask, picked, 0.0), axis=0, keepdims=True)
        prel[bus, s : s + 1, :] = picked * eff
    release = []
    for d in range(1, nbus):
        release.append(send(prel.at[bus], prel.at[bus], s_o.at[d - 1], r_o.at[d - 1], (br, (bus + d) % nbus)))
    for c in release:
        c.wait_recv()
    out = prel[0]
    for b in range(1, nbus):
        out = out + prel[b]
    grel_ref[...] = out
    for c in sends:
        c.wait_send()


def shards(net_load, release, plant_bus, efficiency, ptdf, branch_class, class_limit, class_price):
    nbus = 4
    plants = plant_bus.shape[0]
    classes = class_limit.shape[0]
    branches, columns = ptdf.shape
    tiles = columns // LANES
    tx = 15
    ty = (tiles - NX * tx) // NY
    wx, wy = tx * LANES, ty * LANES
    width = wx + wy
    group = NX * NY
    scen = NZ * group * 2
    bf, f32 = jnp.bfloat16, jnp.float32
    dma = pltpu.SemaphoreType.DMA
    vmem = pl.BlockSpec(memory_space=pltpu.VMEM)
    smem = pl.BlockSpec(memory_space=pltpu.SMEM)
    return pl.pallas_call(
        functools.partial(kernel, (tiles, tx, ty, nbus, plants, classes)),
        out_shape=(
            jax.ShapeDtypeStruct((2, columns), f32),
            jax.ShapeDtypeStruct((2, plants), f32),
        ),
        in_specs=[vmem, vmem, vmem, vmem, pl.BlockSpec(memory_space=pl.ANY), vmem, smem, smem],
        out_specs=(vmem, vmem),
        scratch_shapes=[
            pltpu.VMEM((2, columns), bf),
            pltpu.VMEM((2 * tiles, LANES), f32),
            pltpu.VMEM((NX, branches, wx), bf),
            pltpu.VMEM((NY, branches, wy), bf),
            pltpu.VMEM((group, 2, width), bf),
            pltpu.VMEM((NZ, 2 * group, width), bf),
            pltpu.VMEM((NX + NY, scen, branches), f32),
            pltpu.VMEM((NX, scen, branches), f32),
            pltpu.VMEM((nbus, scen, branches), f32),
            pltpu.VMEM((NX, scen, branches), bf),
            pltpu.VMEM((NY, scen, branches), bf),
            pltpu.VMEM((NZ, 2 * group, width), f32),
            pltpu.VMEM((2, 2, NZ // 2, 2 * group, width), bf),
            pltpu.VMEM((group, 2, width), f32),
            pltpu.VMEM((group, 2, width), f32),
            pltpu.VMEM((2 * tiles, LANES), f32),
            pltpu.VMEM((nbus, 2, plants), f32),
            dma((NX,)), dma((NX,)), dma((2,)),
            dma((2 * (group - 1),)), dma((2 * (group - 1),)), dma((2,)),
            dma((2, NZ // 2, 2)), dma((2, NZ // 2, 2)),
            dma((NX,)), dma((NX,)),
            dma((nbus - 1,)), dma((nbus - 1,)),
            dma((NX,)), dma((NX,)),
            dma((2, NZ // 2, 2)), dma((2, NZ // 2, 2)),
            dma((group - 1,)), dma((group - 1,)),
            dma((nbus - 1,)), dma((nbus - 1,)),
        ],
        compiler_params=pltpu.CompilerParams(
            collective_id=0, has_side_effects=True, vmem_limit_bytes=56 << 20
        ),
    )(
        net_load,
        release,
        plant_bus[None, :],
        efficiency[None, :],
        ptdf,
        branch_class[None, :],
        class_limit,
        class_price,
    )


def solution(mesh):
    placed = (P("br", "bus"), P("br", None), P(), P(), P("br", "bus"), P("br"), P(), P())
    return jax.shard_map(
        shards,
        mesh=mesh,
        in_specs=placed,
        out_specs=(P("br", "bus"), P("br", None)),
        check_vma=False,
    )
```

```python
import functools

import jax
import jax.numpy as jnp
from jax import lax
from jax.experimental import pallas as pl
from jax.experimental.pallas import tpu as pltpu
from jax.sharding import PartitionSpec as P

SMOOTH = 0.25
LANES = 128
NX, NY, NZ = 4, 2, 8
PIECES = 4
MESH = pl.DeviceIdType.MESH
NT = (((1,), (1,)), ((), ()))
TN = (((0,), (0,)), ((), ()))
NN = (((1,), (0,)), ((), ()))


def mm(a, b, dims):
    return lax.dot_general(a, b, dims, preferred_element_type=jnp.float32)


def split3(v):
    one = v.astype(jnp.bfloat16)
    rest = v - one.astype(jnp.float32)
    two = rest.astype(jnp.bfloat16)
    three = (rest - two.astype(jnp.float32)).astype(jnp.bfloat16)
    return one, two, three


def kernel(
    sizes,
    net_ref, rel_ref, plant_ref, eff_ref, ptdf_ref, cls_ref, lim_ref, price_ref,
    gbus_ref, grel_ref,
    inj, acc, px, py, recv_in, xall, fpart, frecv, gx, gy, gpart, ring, sbuf, srecv, rows, prel, hot,
    s_p, r_p, l_p, s_i, r_i, l_i, s_z, r_z, s_f, r_f, s_g, r_g, s_r, r_r, s_s, r_s, s_o, r_o,
):
    tiles, tx, ty, nbus, plants, classes = sizes
    wx, wy = tx * LANES, ty * LANES
    base_y = NX * wx
    width = wx + wy
    part_rows = 2 * NZ * NX * NY // nbus
    third = (ty + 2) // 3 * LANES
    chunks = ((0, wx), (wx, third), (wx + third, third), (wx + 2 * third, wy - 2 * third))
    way = (0, 1, 1, 0)
    br, bus = lax.axis_index("br"), lax.axis_index("bus")
    z, y, x = br // (NX * NY), (br // NX) % NY, br % NX
    me = y * NX + x

    def at(z_, y_, x_):
        return ((z_ * NY + y_) * NX + x_, bus)

    xy_offsets = [(dy, dx) for dy in range(NY) for dx in range(NX) if (dy, dx) != (0, 0)]

    def xy(dy, dx):
        return (y + dy) % NY, (x + dx) % NX

    zup, zdn = (z + 1) % NZ, (z + NZ - 1) % NZ
    partners = [at(z, *xy(dy, dx)) for dy, dx in xy_offsets]
    partners += [at(zup, y, x), at(zdn, y, x)]
    partners += [(br, (bus + d) % nbus) for d in range(1, nbus)]
    yother = (y + 1) % NY
    holders = [(z, y, (x + k) % NX) for k in range(1, NX)] + [(z, yother, x), (z, y, x)]

    def across(j, d):
        z_, y_, x_ = holders[j]
        return ((z_ * NY + y_) * NX + x_, (bus + d) % nbus)

    partners += [across(j, d) for j in range(NX) for d in range(1, nbus)]

    barrier = pltpu.get_barrier_semaphore()
    for p in partners:
        pl.semaphore_signal(barrier, inc=1, device_id=p, device_id_type=MESH)

    sends = []

    def send(src, dst, ss, rs, dev):
        c = pltpu.make_async_remote_copy(
            src_ref=src, dst_ref=dst, send_sem=ss, recv_sem=rs, device_id=dev, device_id_type=MESH
        )
        c.start()
        sends.append(c)
        return c

    def window_x(ref, q):
        return ref.at[:, pl.ds(pl.multiple_of(q * wx, LANES), wx)]

    def window_y(ref, q):
        return ref.at[:, pl.ds(pl.multiple_of(base_y + q * wy, LANES), wy)]

    own_px = pltpu.make_async_copy(window_x(ptdf_ref, x), px.at[x], l_p.at[0])
    own_py = pltpu.make_async_copy(window_y(ptdf_ref, y), py.at[y], l_p.at[1])
    own_px.start()
    own_py.start()
    pl.semaphore_wait(barrier, len(partners))

    factor = []
    piece = ptdf_ref.shape[0] // PIECES

    def factor_piece(p):
        r = pl.ds(p * piece, piece)
        for k in range(1, NX):
            x_ = (x + k) % NX
            factor.append(send(
                ptdf_ref.at[r, pl.ds(pl.multiple_of(x_ * wx, LANES), wx)], px.at[x, r, :],
                s_p.at[k - 1, p], r_p.at[k - 1, p], at(z, y, x_),
            ))
        factor.append(send(
            ptdf_ref.at[r, pl.ds(pl.multiple_of(base_y + yother * wy, LANES), wy)], py.at[y, r, :],
            s_p.at[NX - 1, p], r_p.at[NX - 1, p], at(z, yother, x),
        ))

    col = plant_ref[...] - bus * (tiles * LANES)
    hi = col >> 7
    lo = col & 127
    row_id = lax.broadcasted_iota(jnp.int32, (2 * tiles, plants), 0)
    lo_id = lax.broadcasted_iota(jnp.int32, (LANES, plants), 0)
    lo_hot = (lo_id == lo).astype(jnp.float32).astype(jnp.bfloat16)
    eff = eff_ref[...]
    weight = rel_ref[...] * eff
    here = (row_id >> 1) == hi
    odd = (row_id & 1) == 1
    total = None
    for part in split3(weight):
        part = part.astype(jnp.float32)
        placed = jnp.where(here, jnp.where(odd, part[1:2, :], part[0:1, :]), 0.0)
        term = mm(placed.astype(jnp.bfloat16), lo_hot, NT)
        total = term if total is None else total + term
    acc[...] = total
    for h in range(tiles):
        cols = slice(h * LANES, (h + 1) * LANES)
        inj[:, cols] = (acc[2 * h : 2 * h + 2, :] + net_ref[:, cols].astype(jnp.float32)).astype(jnp.bfloat16)

    arrive_x, arrive_y = [], []
    for k, (dy, dx) in enumerate(xy_offsets):
        y_, x_ = xy(dy, dx)
        arrive_x.append(send(window_x(inj, x_), recv_in.at[me, :, pl.ds(0, wx)], s_i.at[2 * k], r_i.at[2 * k], at(z, y_, x_)))
    own_ix = pltpu.make_async_copy(window_x(inj, x), recv_in.at[me, :, pl.ds(0, wx)], l_i.at[0])
    own_ix.start()
    for k, (dy, dx) in enumerate(xy_offsets):
        y_, x_ = xy(dy, dx)
        arrive_y.append(send(window_y(inj, y_), recv_in.at[me, :, pl.ds(wx, wy)], s_i.at[2 * k + 1], r_i.at[2 * k + 1], at(z, y_, x_)))
    own_iy = pltpu.make_async_copy(window_y(inj, y), recv_in.at[me, :, pl.ds(wx, wy)], l_i.at[1])
    own_iy.start()
    factor_piece(0)

    cls = cls_ref[...]
    limit = jnp.zeros(cls.shape, jnp.float32)
    price = jnp.zeros(cls.shape, jnp.float32)
    for k in range(classes):
        limit = jnp.where(cls == k, lim_ref[k], limit)
        price = jnp.where(cls == k, price_ref[k], price)

    for s in range(2):
        hot[s] = jnp.where(here & (odd == (s == 1)), 1.0, 0.0).astype(jnp.bfloat16)
    flight = {}

    def ring_gather(step, d, c):
        start, size = chunks[c]
        if step > 1:
            flight[step - 1, d, c].wait_recv()
        n = (z + NZ - (step - 1)) % NZ if d == 0 else (z + (step - 1)) % NZ
        block = xall.at[n, :, pl.ds(start, size)]
        flight[step, d, c] = send(block, block, s_z.at[d, step - 1, c], r_z.at[d, step - 1, c], at(zup if d == 0 else zdn, y, x))

    own_ix.wait()
    for c in arrive_x:
        c.wait_recv()
    for i in range(NX * NY):
        xall[z, 2 * i : 2 * i + 2, 0:wx] = recv_in[i, :, 0:wx]
    for d in range(2):
        ring_gather(1, d, 0)
    own_iy.wait()
    for c in arrive_y:
        c.wait_recv()
    for i in range(NX * NY):
        xall[z, 2 * i : 2 * i + 2, wx:width] = recv_in[i, :, wx:width]
    for c in range(1, len(chunks)):
        for d in range(2):
            ring_gather(1, d, c)
    factor_piece(1)
    half = NZ // 2
    for step in range(2, half):
        for c in range(len(chunks)):
            for d in range(2):
                ring_gather(step, d, c)
        if step == 2:
            for p in range(2, PIECES):
                factor_piece(p)
    for c in range(len(chunks)):
        ring_gather(half, way[c], c)
    for c in range(len(chunks)):
        flight[half - 1, 1 - way[c], c].wait_recv()
        flight[half, way[c], c].wait_recv()

    own_px.wait()
    own_py.wait()
    for c in factor:
        c.wait_recv()
    scen = NZ * 2 * NX * NY
    lhs_x = xall[:, :, 0:wx].reshape(scen, wx)
    for q in range(NX):
        fpart[q] = mm(lhs_x, px[q], NT)
    lhs_y = xall[:, :, wx:width].reshape(scen, wy)
    for q in range(NY):
        fpart[NX + q] = mm(lhs_y, py[q], NT)

    def quarter(d):
        return pl.ds(pl.multiple_of((bus + d) % nbus * part_rows, part_rows), part_rows)

    slots = [(x + k) % NX for k in range(1, NX)] + [NX + yother, x]
    fpart[x] = fpart[x] + fpart[NX + y]
    back = []
    for j in range(NX + 1):
        for d in range(nbus):
            if (j, d) != (NX, 0):
                back.append(send(fpart.at[slots[j], quarter(d), :], frecv.at[j, d], s_f.at[j, d], r_f.at[j, d], across(j, d)))
    flows = fpart[x, quarter(0), :]
    for c in back:
        c.wait_recv()
    for j in range(NX + 1):
        for d in range(nbus):
            if (j, d) != (NX, 0):
                flows = flows + frecv[j, d]
    upper = jax.nn.sigmoid((flows - limit) / SMOOTH)
    lower = jax.nn.sigmoid((-flows - limit) / SMOOTH)
    gx[x, quarter(0), :] = (price * (upper - lower)).astype(jnp.bfloat16)
    given = []
    mine = gx.at[x, quarter(0), :]
    for j in range(NX + 1):
        for d in range(nbus):
            if (j, d) != (NX, 0):
                there = gy.at[y, quarter(0), :] if j == NX - 1 else mine
                given.append(send(mine, there, s_g.at[j, d], r_g.at[j, d], across(j, d)))
    for c in given:
        c.wait_recv()
    gy[y] = gx[x]

    def product(g, p, n):
        total = mm(g[0], p[0], NN)
        for q in range(1, n):
            total = total + mm(g[q], p[q], NN)
        return total.reshape(NZ, scen // NZ, p.shape[2])

    down = {}

    def ring_reduce(step, d, c):
        start, size = chunks[c]
        away = half + 1 - step
        target = (z + away) % NZ if d == 0 else (z + NZ - away) % NZ
        value = gpart[target, :, start : start + size]
        if (step - 1, d, c) in down:
            down[step - 1, d, c].wait_recv()
            value = value + ring[1, d, step - 2, :, start : start + size].astype(jnp.float32)
        ring[0, d, step - 1, :, start : start + size] = value.astype(jnp.bfloat16)
        down[step, d, c] = send(
            ring.at[0, d, step - 1, :, pl.ds(start, size)],
            ring.at[1, d, step - 1, :, pl.ds(start, size)],
            s_r.at[d, step - 1, c], r_r.at[d, step - 1, c],
            at(zup if d == 0 else zdn, y, x),
        )

    order = (1, 2, 3, 0)
    gpart[:, :, wx:width] = product(gy, py, NY)
    for c in order:
        if c == 0:
            gpart[:, :, 0:wx] = product(gx, px, NX)
        ring_reduce(1, way[c], c)
        ring_reduce(2, 1 - way[c], c)
    for c in order:
        ring_reduce(2, way[c], c)
    for step in range(3, half + 1):
        for c in order:
            ring_reduce(step, 1 - way[c], c)
        for c in order:
            ring_reduce(step, way[c], c)
    last = []
    for c in order:
        start, size = chunks[c]
        value = gpart[z, :, start : start + size]
        for d in range(2):
            down[half, d, c].wait_recv()
            value = value + ring[1, d, half - 1, :, start : start + size].astype(jnp.float32)
        for i in range(NX * NY):
            sbuf[i, :, start : start + size] = value[2 * i : 2 * i + 2, :]
        if c in (3, 0):
            start, size = (0, wx) if c == 0 else (wx, wy)
            for k, (dy, dx) in enumerate(xy_offsets):
                y2, x2 = xy(dy, dx)
                last.append(send(
                    sbuf.at[y2 * NX + x2, :, pl.ds(start, size)], srecv.at[me, :, pl.ds(start, size)],
                    s_s.at[k, c % 2], r_s.at[k, c % 2], at(z, y2, x2),
                ))
    srecv[me] = sbuf[me]
    for c in last:
        c.wait_recv()
    for q in range(NX):
        part = srecv[q, :, 0:wx]
        for j in range(1, NY):
            part = part + srecv[j * NX + q, :, 0:wx]
        gbus_ref[:, q * wx : (q + 1) * wx] = part
    for q in range(NY):
        part = srecv[q * NX, :, wx:width]
        for j in range(1, NX):
            part = part + srecv[q * NX + j, :, wx:width]
        gbus_ref[:, base_y + q * wy : base_y + (q + 1) * wy] = part

    for h in range(tiles):
        rows[2 * h : 2 * h + 2, :] = gbus_ref[:, h * LANES : (h + 1) * LANES]
    parts = jnp.concatenate(split3(rows[...]), axis=1)
    lo_mask = lo_id == lo
    for s in range(2):
        picked = mm(parts, hot[s], TN)
        picked = picked[0:LANES] + picked[LANES : 2 * LANES] + picked[2 * LANES :]
        picked = jnp.sum(jnp.where(lo_mask, picked, 0.0), axis=0, keepdims=True)
        prel[bus, s : s + 1, :] = picked * eff
    release = []
    for d in range(1, nbus):
        release.append(send(prel.at[bus], prel.at[bus], s_o.at[d - 1], r_o.at[d - 1], (br, (bus + d) % nbus)))
    for c in release:
        c.wait_recv()
    out = prel[0]
    for b in range(1, nbus):
        out = out + prel[b]
    grel_ref[...] = out
    for c in sends:
        c.wait_send()


def shards(net_load, release, plant_bus, efficiency, ptdf, branch_class, class_limit, class_price):
    nbus = 4
    plants = plant_bus.shape[0]
    classes = class_limit.shape[0]
    branches, columns = ptdf.shape
    tiles = columns // LANES
    tx = 15
    ty = (tiles - NX * tx) // NY
    wx, wy = tx * LANES, ty * LANES
    width = wx + wy
    group = NX * NY
    scen = NZ * group * 2
    bf, f32 = jnp.bfloat16, jnp.float32
    dma = pltpu.SemaphoreType.DMA
    vmem = pl.BlockSpec(memory_space=pltpu.VMEM)
    smem = pl.BlockSpec(memory_space=pltpu.SMEM)
    return pl.pallas_call(
        functools.partial(kernel, (tiles, tx, ty, nbus, plants, classes)),
        out_shape=(
            jax.ShapeDtypeStruct((2, columns), f32),
            jax.ShapeDtypeStruct((2, plants), f32),
        ),
        in_specs=[vmem, vmem, vmem, vmem, pl.BlockSpec(memory_space=pl.ANY), vmem, smem, smem],
        out_specs=(vmem, vmem),
        scratch_shapes=[
            pltpu.VMEM((2, columns), bf),
            pltpu.VMEM((2 * tiles, LANES), f32),
            pltpu.VMEM((NX, branches, wx), bf),
            pltpu.VMEM((NY, branches, wy), bf),
            pltpu.VMEM((group, 2, width), bf),
            pltpu.VMEM((NZ, 2 * group, width), bf),
            pltpu.VMEM((NX + NY, scen, branches), f32),
            pltpu.VMEM((NX + 1, nbus, scen // nbus, branches), f32),
            pltpu.VMEM((NX, scen, branches), bf),
            pltpu.VMEM((NY, scen, branches), bf),
            pltpu.VMEM((NZ, 2 * group, width), f32),
            pltpu.VMEM((2, 2, NZ // 2, 2 * group, width), bf),
            pltpu.VMEM((group, 2, width), f32),
            pltpu.VMEM((group, 2, width), f32),
            pltpu.VMEM((2 * tiles, LANES), f32),
            pltpu.VMEM((nbus, 2, plants), f32),
            pltpu.VMEM((2, 2 * tiles, plants), bf),
            dma((NX, PIECES)), dma((NX, PIECES)), dma((2,)),
            dma((2 * (group - 1),)), dma((2 * (group - 1),)), dma((2,)),
            dma((2, NZ // 2, 4)), dma((2, NZ // 2, 4)),
            dma((NX + 1, nbus)), dma((NX + 1, nbus)),
            dma((NX + 1, nbus)), dma((NX + 1, nbus)),
            dma((2, NZ // 2, 4)), dma((2, NZ // 2, 4)),
            dma((group - 1, 2)), dma((group - 1, 2)),
            dma((nbus - 1,)), dma((nbus - 1,)),
        ],
        compiler_params=pltpu.CompilerParams(
            collective_id=0, has_side_effects=True, vmem_limit_bytes=56 << 20
        ),
    )(
        net_load,
        release,
        plant_bus[None, :],
        efficiency[None, :],
        ptdf,
        branch_class[None, :],
        class_limit,
        class_price,
    )


def solution(mesh):
    placed = (P("br", "bus"), P("br", None), P(), P(), P("br", "bus"), P("br"), P(), P())
    return jax.shard_map(
        shards,
        mesh=mesh,
        in_specs=placed,
        out_specs=(P("br", "bus"), P("br", None)),
        check_vma=False,
    )
```

```python
import functools

import jax
import jax.numpy as jnp
from jax import lax
from jax.experimental import pallas as pl
from jax.experimental.pallas import tpu as pltpu
from jax.sharding import PartitionSpec as P

SMOOTH = 0.25
LANES = 128
NX, NY, NZ = 4, 2, 8
PIECES = 4
MESH = pl.DeviceIdType.MESH
NT = (((1,), (1,)), ((), ()))
TN = (((0,), (0,)), ((), ()))
NN = (((1,), (0,)), ((), ()))


def mm(a, b, dims):
    return lax.dot_general(a, b, dims, preferred_element_type=jnp.float32)


def split3(v):
    one = v.astype(jnp.bfloat16)
    rest = v - one.astype(jnp.float32)
    two = rest.astype(jnp.bfloat16)
    three = (rest - two.astype(jnp.float32)).astype(jnp.bfloat16)
    return one, two, three


def kernel(
    sizes,
    net_in, rel_in, plant_in, eff_in, ptdf_ref, cls_in, lim_in, price_in,
    gbus_ref, grel_ref,
    net_ref, rel_ref, plant_ref, eff_ref, cls_ref, lim_ref, price_ref,
    inj, acc, px, py, recv_in, xall, fpart, frecv, gx, gy, gpart, ring, sbuf, srecv, rows, prel, hot,
    l_in, s_p, r_p, l_p, s_i, r_i, l_i, s_z, r_z, s_f, r_f, s_g, r_g, s_r, r_r, s_s, r_s, s_o, r_o,
):
    tiles, tx, ty, nbus, plants, classes = sizes
    wx, wy = tx * LANES, ty * LANES
    base_y = NX * wx
    width = wx + wy
    part_rows = 2 * NZ * NX * NY // nbus
    third = (ty + 2) // 3 * LANES
    chunks = ((0, wx), (wx, third), (wx + third, third), (wx + 2 * third, wy - 2 * third))
    way = (0, 1, 1, 0)
    br, bus = lax.axis_index("br"), lax.axis_index("bus")
    z, y, x = br // (NX * NY), (br // NX) % NY, br % NX
    me = y * NX + x

    def at(z_, y_, x_):
        return ((z_ * NY + y_) * NX + x_, bus)

    xy_offsets = [(dy, dx) for dy in range(NY) for dx in range(NX) if (dy, dx) != (0, 0)]

    def xy(dy, dx):
        return (y + dy) % NY, (x + dx) % NX

    zup, zdn = (z + 1) % NZ, (z + NZ - 1) % NZ
    partners = [at(z, *xy(dy, dx)) for dy, dx in xy_offsets]
    partners += [at(zup, y, x), at(zdn, y, x)]
    partners += [(br, (bus + d) % nbus) for d in range(1, nbus)]
    yother = (y + 1) % NY
    holders = [(z, y, (x + k) % NX) for k in range(1, NX)] + [(z, yother, x), (z, y, x)]

    def across(j, d):
        z_, y_, x_ = holders[j]
        return ((z_ * NY + y_) * NX + x_, (bus + d) % nbus)

    partners += [across(j, d) for j in range(NX) for d in range(1, nbus)]

    barrier = pltpu.get_barrier_semaphore()
    for p in partners:
        pl.semaphore_signal(barrier, inc=1, device_id=p, device_id_type=MESH)

    loads = [
        pltpu.make_async_copy(src, dst, l_in.at[i])
        for i, (src, dst) in enumerate((
            (plant_in, plant_ref), (rel_in, rel_ref), (eff_in, eff_ref), (net_in, net_ref),
            (cls_in, cls_ref), (lim_in, lim_ref), (price_in, price_ref),
        ))
    ]
    for c in loads:
        c.start()

    sends = []

    def send(src, dst, ss, rs, dev):
        c = pltpu.make_async_remote_copy(
            src_ref=src, dst_ref=dst, send_sem=ss, recv_sem=rs, device_id=dev, device_id_type=MESH
        )
        c.start()
        sends.append(c)
        return c

    def window_x(ref, q):
        return ref.at[:, pl.ds(pl.multiple_of(q * wx, LANES), wx)]

    def window_y(ref, q):
        return ref.at[:, pl.ds(pl.multiple_of(base_y + q * wy, LANES), wy)]

    own_px = pltpu.make_async_copy(window_x(ptdf_ref, x), px.at[x], l_p.at[0])
    own_py = pltpu.make_async_copy(window_y(ptdf_ref, y), py.at[y], l_p.at[1])
    own_px.start()
    own_py.start()

    for c in loads:
        c.wait()
    factor = []
    piece = ptdf_ref.shape[0] // PIECES

    def factor_piece(p):
        r = pl.ds(p * piece, piece)
        for k in range(1, NX):
            x_ = (x + k) % NX
            factor.append(send(
                ptdf_ref.at[r, pl.ds(pl.multiple_of(x_ * wx, LANES), wx)], px.at[x, r, :],
                s_p.at[k - 1, p], r_p.at[k - 1, p], at(z, y, x_),
            ))
        factor.append(send(
            ptdf_ref.at[r, pl.ds(pl.multiple_of(base_y + yother * wy, LANES), wy)], py.at[y, r, :],
            s_p.at[NX - 1, p], r_p.at[NX - 1, p], at(z, yother, x),
        ))

    col = plant_ref[...] - bus * (tiles * LANES)
    hi = col >> 7
    lo = col & 127
    row_id = lax.broadcasted_iota(jnp.int32, (2 * tiles, plants), 0)
    lo_id = lax.broadcasted_iota(jnp.int32, (LANES, plants), 0)
    lo_hot = (lo_id == lo).astype(jnp.float32).astype(jnp.bfloat16)
    eff = eff_ref[...]
    weight = rel_ref[...] * eff
    here = (row_id >> 1) == hi
    odd = (row_id & 1) == 1
    total = None
    for part in split3(weight):
        part = part.astype(jnp.float32)
        placed = jnp.where(here, jnp.where(odd, part[1:2, :], part[0:1, :]), 0.0)
        term = mm(placed.astype(jnp.bfloat16), lo_hot, NT)
        total = term if total is None else total + term
    acc[...] = total
    for h in range(tiles):
        cols = slice(h * LANES, (h + 1) * LANES)
        inj[:, cols] = (acc[2 * h : 2 * h + 2, :] + net_ref[:, cols].astype(jnp.float32)).astype(jnp.bfloat16)

    pl.semaphore_wait(barrier, len(partners))
    arrive_x, arrive_y = [], []
    for k, (dy, dx) in enumerate(xy_offsets):
        y_, x_ = xy(dy, dx)
        arrive_x.append(send(window_x(inj, x_), recv_in.at[me, :, pl.ds(0, wx)], s_i.at[2 * k], r_i.at[2 * k], at(z, y_, x_)))
    own_ix = pltpu.make_async_copy(window_x(inj, x), recv_in.at[me, :, pl.ds(0, wx)], l_i.at[0])
    own_ix.start()
    for k, (dy, dx) in enumerate(xy_offsets):
        y_, x_ = xy(dy, dx)
        arrive_y.append(send(window_y(inj, y_), recv_in.at[me, :, pl.ds(wx, wy)], s_i.at[2 * k + 1], r_i.at[2 * k + 1], at(z, y_, x_)))
    own_iy = pltpu.make_async_copy(window_y(inj, y), recv_in.at[me, :, pl.ds(wx, wy)], l_i.at[1])
    own_iy.start()
    factor_piece(0)

    cls = cls_ref[...]
    limit = jnp.zeros(cls.shape, jnp.float32)
    price = jnp.zeros(cls.shape, jnp.float32)
    for k in range(classes):
        limit = jnp.where(cls == k, lim_ref[:, k : k + 1], limit)
        price = jnp.where(cls == k, price_ref[:, k : k + 1], price)

    for s in range(2):
        hot[s] = jnp.where(here & (odd == (s == 1)), 1.0, 0.0).astype(jnp.bfloat16)
    flight = {}

    def ring_gather(step, d, c):
        start, size = chunks[c]
        if step > 1:
            flight[step - 1, d, c].wait_recv()
        n = (z + NZ - (step - 1)) % NZ if d == 0 else (z + (step - 1)) % NZ
        block = xall.at[n, :, pl.ds(start, size)]
        flight[step, d, c] = send(block, block, s_z.at[d, step - 1, c], r_z.at[d, step - 1, c], at(zup if d == 0 else zdn, y, x))

    own_ix.wait()
    for c in arrive_x:
        c.wait_recv()
    for i in range(NX * NY):
        xall[z, 2 * i : 2 * i + 2, 0:wx] = recv_in[i, :, 0:wx]
    for d in range(2):
        ring_gather(1, d, 0)
    own_iy.wait()
    for c in arrive_y:
        c.wait_recv()
    for i in range(NX * NY):
        xall[z, 2 * i : 2 * i + 2, wx:width] = recv_in[i, :, wx:width]
    for c in range(1, len(chunks)):
        for d in range(2):
            ring_gather(1, d, c)
    factor_piece(1)
    half = NZ // 2
    for step in range(2, half):
        for c in range(len(chunks)):
            for d in range(2):
                ring_gather(step, d, c)
        if step == 2:
            for p in range(2, PIECES):
                factor_piece(p)
    for c in range(len(chunks)):
        ring_gather(half, way[c], c)
    for c in range(len(chunks)):
        flight[half - 1, 1 - way[c], c].wait_recv()
        flight[half, way[c], c].wait_recv()

    own_px.wait()
    own_py.wait()
    for c in factor:
        c.wait_recv()
    scen = NZ * 2 * NX * NY
    branches = ptdf_ref.shape[0]
    scen = NZ * 2 * NX * NY
    def quarter(d):
        return pl.ds(pl.multiple_of((bus + d) % nbus * part_rows, part_rows), part_rows)

    slots = [(x + k) % NX for k in range(1, NX)] + [NX + yother, x]
    back = []

    def to_holder(j):
        for d in range(nbus):
            if (j, d) != (NX, 0):
                back.append(send(fpart.at[slots[j], quarter(d), :], frecv.at[j, d], s_f.at[j, d], r_f.at[j, d], across(j, d)))

    part = mm(xall[:, :, 0:wx].reshape(scen, wx), px[...].reshape(NX * branches, wx), NT)
    for q in range(NX):
        fpart[q] = part[:, q * branches : (q + 1) * branches]
    for j in range(NX - 1):
        to_holder(j)
    part = mm(xall[:, :, wx:width].reshape(scen, wy), py[...].reshape(NY * branches, wy), NT)
    for q in range(NY):
        fpart[NX + q] = part[:, q * branches : (q + 1) * branches]
    to_holder(NX - 1)
    fpart[x] = fpart[x] + fpart[NX + y]
    to_holder(NX)
    flows = fpart[x, quarter(0), :]
    for c in back:
        c.wait_recv()
    for j in range(NX + 1):
        for d in range(nbus):
            if (j, d) != (NX, 0):
                flows = flows + frecv[j, d]
    upper = jax.nn.sigmoid((flows - limit) / SMOOTH)
    lower = jax.nn.sigmoid((-flows - limit) / SMOOTH)
    gx[x, quarter(0), :] = (price * (upper - lower)).astype(jnp.bfloat16)
    given = {}
    mine = gx.at[x, quarter(0), :]
    for j in (NX, NX - 1, 0, 1, 2):
        there = gy.at[y, quarter(0), :] if j == NX - 1 else mine
        given[j] = [
            send(mine, there, s_g.at[j, d], r_g.at[j, d], across(j, d)) for d in range(nbus) if (j, d) != (NX, 0)
        ]
    for j in (NX, NX - 1):
        for c in given[j]:
            c.wait_recv()
    gy[y] = gx[x]

    def product(g, p, n):
        lhs = jnp.concatenate([g[q] for q in range(n)], axis=1)
        total = mm(lhs, p[...].reshape(n * branches, p.shape[2]), NN)
        return total.reshape(NZ, scen // NZ, p.shape[2])

    down = {}

    def ring_reduce(step, d, c):
        start, size = chunks[c]
        away = half + 1 - step
        target = (z + away) % NZ if d == 0 else (z + NZ - away) % NZ
        value = gpart[target, :, start : start + size]
        if (step - 1, d, c) in down:
            down[step - 1, d, c].wait_recv()
            value = value + ring[1, d, step - 2, :, start : start + size].astype(jnp.float32)
        ring[0, d, step - 1, :, start : start + size] = value.astype(jnp.bfloat16)
        down[step, d, c] = send(
            ring.at[0, d, step - 1, :, pl.ds(start, size)],
            ring.at[1, d, step - 1, :, pl.ds(start, size)],
            s_r.at[d, step - 1, c], r_r.at[d, step - 1, c],
            at(zup if d == 0 else zdn, y, x),
        )

    order = (1, 2, 3, 0)
    gpart[:, :, wx:width] = product(gy, py, NY)
    for c in order:
        if c == 0:
            for j in range(NX - 1):
                for arrived in given[j]:
                    arrived.wait_recv()
            gpart[:, :, 0:wx] = product(gx, px, NX)
        ring_reduce(1, way[c], c)
        ring_reduce(2, 1 - way[c], c)
    for c in order:
        ring_reduce(2, way[c], c)
    for step in range(3, half + 1):
        for c in order:
            ring_reduce(step, 1 - way[c], c)
        for c in order:
            ring_reduce(step, way[c], c)
    last = []
    for c in order:
        start, size = chunks[c]
        value = gpart[z, :, start : start + size]
        for d in range(2):
            down[half, d, c].wait_recv()
            value = value + ring[1, d, half - 1, :, start : start + size].astype(jnp.float32)
        for i in range(NX * NY):
            sbuf[i, :, start : start + size] = value[2 * i : 2 * i + 2, :]
        if c in (3, 0):
            start, size = (0, wx) if c == 0 else (wx, wy)
            for k, (dy, dx) in enumerate(xy_offsets):
                y2, x2 = xy(dy, dx)
                last.append(send(
                    sbuf.at[y2 * NX + x2, :, pl.ds(start, size)], srecv.at[me, :, pl.ds(start, size)],
                    s_s.at[k, c % 2], r_s.at[k, c % 2], at(z, y2, x2),
                ))
    srecv[me] = sbuf[me]

    def pick(first, count):
        for h in range(first, first + count):
            rows[2 * h : 2 * h + 2, :] = gbus_ref[:, h * LANES : (h + 1) * LANES]
        parts = jnp.concatenate(split3(rows[2 * first : 2 * (first + count), :]), axis=1)
        both = []
        for s in range(2):
            picked = mm(parts, hot[s, 2 * first : 2 * (first + count), :], TN)
            both.append(picked[0:LANES] + picked[LANES : 2 * LANES] + picked[2 * LANES :])
        return both

    for c in last[: NX * NY - 1]:
        c.wait_recv()
    for q in range(NY):
        part = srecv[q * NX, :, wx:width]
        for j in range(1, NX):
            part = part + srecv[q * NX + j, :, wx:width]
        gbus_ref[:, base_y + q * wy : base_y + (q + 1) * wy] = part
    picked_y = pick(NX * tx, NY * ty)
    for c in last[NX * NY - 1 :]:
        c.wait_recv()
    for q in range(NX):
        part = srecv[q, :, 0:wx]
        for j in range(1, NY):
            part = part + srecv[j * NX + q, :, 0:wx]
        gbus_ref[:, q * wx : (q + 1) * wx] = part
    picked_x = pick(0, NX * tx)
    lo_mask = lo_id == lo
    for s in range(2):
        picked = jnp.sum(jnp.where(lo_mask, picked_x[s] + picked_y[s], 0.0), axis=0, keepdims=True)
        prel[bus, s : s + 1, :] = picked * eff
    release = []
    for d in range(1, nbus):
        release.append(send(prel.at[bus], prel.at[bus], s_o.at[d - 1], r_o.at[d - 1], (br, (bus + d) % nbus)))
    for c in release:
        c.wait_recv()
    out = prel[0]
    for b in range(1, nbus):
        out = out + prel[b]
    grel_ref[...] = out
    for c in sends:
        c.wait_send()


def finish(gbus_in, grel_in, gbus_ref, grel_ref):
    gbus_ref[...] = gbus_in[...]
    grel_ref[...] = grel_in[...]


def shards(net_load, release, plant_bus, efficiency, ptdf, branch_class, class_limit, class_price):
    nbus = 4
    plants = plant_bus.shape[0]
    classes = class_limit.shape[0]
    branches, columns = ptdf.shape
    tiles = columns // LANES
    tx = 15
    ty = (tiles - NX * tx) // NY
    wx, wy = tx * LANES, ty * LANES
    width = wx + wy
    group = NX * NY
    scen = NZ * group * 2
    bf, f32 = jnp.bfloat16, jnp.float32
    dma = pltpu.SemaphoreType.DMA
    vmem = pl.BlockSpec(memory_space=pltpu.VMEM)
    out = pl.pallas_call(
        functools.partial(kernel, (tiles, tx, ty, nbus, plants, classes)),
        out_shape=(
            jax.ShapeDtypeStruct((2, columns), f32),
            jax.ShapeDtypeStruct((2, plants), f32),
        ),
        in_specs=[pl.BlockSpec(memory_space=pl.ANY)] * 8,
        out_specs=(vmem, vmem),
        scratch_shapes=[
            pltpu.VMEM((2, columns), bf),
            pltpu.VMEM((2, plants), f32),
            pltpu.VMEM((1, plants), jnp.int32),
            pltpu.VMEM((1, plants), f32),
            pltpu.VMEM((1, branches), jnp.int32),
            pltpu.VMEM((1, classes), f32),
            pltpu.VMEM((1, classes), f32),
            pltpu.VMEM((2, columns), bf),
            pltpu.VMEM((2 * tiles, LANES), f32),
            pltpu.VMEM((NX, branches, wx), bf),
            pltpu.VMEM((NY, branches, wy), bf),
            pltpu.VMEM((group, 2, width), bf),
            pltpu.VMEM((NZ, 2 * group, width), bf),
            pltpu.VMEM((NX + NY, scen, branches), f32),
            pltpu.VMEM((NX + 1, nbus, scen // nbus, branches), f32),
            pltpu.VMEM((NX, scen, branches), bf),
            pltpu.VMEM((NY, scen, branches), bf),
            pltpu.VMEM((NZ, 2 * group, width), f32),
            pltpu.VMEM((2, 2, NZ // 2, 2 * group, width), bf),
            pltpu.VMEM((group, 2, width), f32),
            pltpu.VMEM((group, 2, width), f32),
            pltpu.VMEM((2 * tiles, LANES), f32),
            pltpu.VMEM((nbus, 2, plants), f32),
            pltpu.VMEM((2, 2 * tiles, plants), bf),
            dma((7,)), dma((NX, PIECES)), dma((NX, PIECES)), dma((2,)),
            dma((2 * (group - 1),)), dma((2 * (group - 1),)), dma((2,)),
            dma((2, NZ // 2, 4)), dma((2, NZ // 2, 4)),
            dma((NX + 1, nbus)), dma((NX + 1, nbus)),
            dma((NX + 1, nbus)), dma((NX + 1, nbus)),
            dma((2, NZ // 2, 4)), dma((2, NZ // 2, 4)),
            dma((group - 1, 2)), dma((group - 1, 2)),
            dma((nbus - 1,)), dma((nbus - 1,)),
        ],
        compiler_params=pltpu.CompilerParams(
            collective_id=0, has_side_effects=True, vmem_limit_bytes=56 << 20
        ),
    )(
        net_load,
        release,
        plant_bus[None, :],
        efficiency[None, :],
        ptdf,
        branch_class[None, :],
        class_limit[None, :],
        class_price[None, :],
    )
    return pl.pallas_call(
        finish,
        out_shape=(jax.ShapeDtypeStruct((2, columns), f32), jax.ShapeDtypeStruct((2, plants), f32)),
        in_specs=[vmem] * 2,
        out_specs=(vmem, vmem),
    )(*out)


def solution(mesh):
    placed = (P("br", "bus"), P("br", None), P(), P(), P("br", "bus"), P("br"), P(), P())
    return jax.shard_map(
        shards,
        mesh=mesh,
        in_specs=placed,
        out_specs=(P("br", "bus"), P("br", None)),
        check_vma=False,
    )
```

```python
import functools

import jax
import jax.numpy as jnp
from jax import lax
from jax.experimental import pallas as pl
from jax.experimental.pallas import tpu as pltpu
from jax.sharding import PartitionSpec as P

SMOOTH = 0.25
LANES = 128
NX, NY, NZ = 4, 2, 8
PIECES = 4
MESH = pl.DeviceIdType.MESH
NT = (((1,), (1,)), ((), ()))
TN = (((0,), (0,)), ((), ()))
NN = (((1,), (0,)), ((), ()))


def mm(a, b, dims):
    return lax.dot_general(a, b, dims, preferred_element_type=jnp.float32)


def split3(v):
    one = v.astype(jnp.bfloat16)
    rest = v - one.astype(jnp.float32)
    two = rest.astype(jnp.bfloat16)
    three = (rest - two.astype(jnp.float32)).astype(jnp.bfloat16)
    return one, two, three


def kernel(
    sizes,
    net_in, rel_in, plant_in, eff_in, ptdf_ref, cls_in, lim_in, price_in,
    gbus_ref, grel_ref,
    net_ref, rel_ref, plant_ref, eff_ref, cls_ref, lim_ref, price_ref,
    inj, acc, px, py, recv_in, xall, fpart, frecv, gx, gy, gpart, ring, sbuf, srecv, rows, prel, hot,
    l_in, s_p, r_p, l_p, s_i, r_i, l_i, s_z, r_z, s_f, r_f, s_g, r_g, s_r, r_r, s_s, r_s, s_o, r_o,
):
    tiles, tx, ty, nbus, plants, classes = sizes
    wx, wy = tx * LANES, ty * LANES
    base_y = NX * wx
    width = wx + wy
    part_rows = 2 * NZ * NX * NY // nbus
    third = (ty + 2) // 3 * LANES
    chunks = ((0, wx), (wx, third), (wx + third, third), (wx + 2 * third, wy - 2 * third))
    way = (1, 0, 0, 1)
    br, bus = lax.axis_index("br"), lax.axis_index("bus")
    z, y, x = br // (NX * NY), (br // NX) % NY, br % NX
    me = y * NX + x

    def at(z_, y_, x_):
        return ((z_ * NY + y_) * NX + x_, bus)

    xy_offsets = [(dy, dx) for dy in range(NY) for dx in range(NX) if (dy, dx) != (0, 0)]

    def xy(dy, dx):
        return (y + dy) % NY, (x + dx) % NX

    zup, zdn = (z + 1) % NZ, (z + NZ - 1) % NZ
    partners = [at(z, *xy(dy, dx)) for dy, dx in xy_offsets]
    partners += [at(zup, y, x), at(zdn, y, x)]
    partners += [(br, (bus + d) % nbus) for d in range(1, nbus)]
    yother = (y + 1) % NY
    holders = [(z, y, (x + k) % NX) for k in range(1, NX)] + [(z, yother, x), (z, y, x)]

    def across(j, d):
        z_, y_, x_ = holders[j]
        return ((z_ * NY + y_) * NX + x_, (bus + d) % nbus)

    partners += [across(j, d) for j in range(NX) for d in range(1, nbus)]

    barrier = pltpu.get_barrier_semaphore()
    for p in partners:
        pl.semaphore_signal(barrier, inc=1, device_id=p, device_id_type=MESH)

    loads = [
        pltpu.make_async_copy(src, dst, l_in.at[i])
        for i, (src, dst) in enumerate((
            (plant_in, plant_ref), (rel_in, rel_ref), (eff_in, eff_ref), (net_in, net_ref),
            (cls_in, cls_ref), (lim_in, lim_ref), (price_in, price_ref),
        ))
    ]
    for c in loads:
        c.start()

    sends = []

    def send(src, dst, ss, rs, dev):
        c = pltpu.make_async_remote_copy(
            src_ref=src, dst_ref=dst, send_sem=ss, recv_sem=rs, device_id=dev, device_id_type=MESH
        )
        c.start()
        sends.append(c)
        return c

    def window_x(ref, q):
        return ref.at[:, pl.ds(pl.multiple_of(q * wx, LANES), wx)]

    def window_y(ref, q):
        return ref.at[:, pl.ds(pl.multiple_of(base_y + q * wy, LANES), wy)]

    own_px = pltpu.make_async_copy(window_x(ptdf_ref, x), px.at[x], l_p.at[0])
    own_py = pltpu.make_async_copy(window_y(ptdf_ref, y), py.at[y], l_p.at[1])
    own_px.start()
    own_py.start()

    for c in loads:
        c.wait()
    factor = []
    piece = ptdf_ref.shape[0] // PIECES

    def factor_piece(p):
        r = pl.ds(p * piece, piece)
        for k in (2, 1, 3):
            x_ = (x + k) % NX
            factor.append(send(
                ptdf_ref.at[r, pl.ds(pl.multiple_of(x_ * wx, LANES), wx)], px.at[x, r, :],
                s_p.at[k - 1, p], r_p.at[k - 1, p], at(z, y, x_),
            ))
        factor.append(send(
            ptdf_ref.at[r, pl.ds(pl.multiple_of(base_y + yother * wy, LANES), wy)], py.at[y, r, :],
            s_p.at[NX - 1, p], r_p.at[NX - 1, p], at(z, yother, x),
        ))

    col = plant_ref[...] - bus * (tiles * LANES)
    hi = col >> 7
    lo = col & 127
    row_id = lax.broadcasted_iota(jnp.int32, (2 * tiles, plants), 0)
    lo_id = lax.broadcasted_iota(jnp.int32, (LANES, plants), 0)
    lo_hot = (lo_id == lo).astype(jnp.float32).astype(jnp.bfloat16)
    eff = eff_ref[...]
    weight = rel_ref[...] * eff
    here = (row_id >> 1) == hi
    odd = (row_id & 1) == 1
    total = None
    for part in split3(weight):
        part = part.astype(jnp.float32)
        placed = jnp.where(here, jnp.where(odd, part[1:2, :], part[0:1, :]), 0.0)
        term = mm(placed.astype(jnp.bfloat16), lo_hot, NT)
        total = term if total is None else total + term
    acc[...] = total
    for h in range(tiles):
        cols = slice(h * LANES, (h + 1) * LANES)
        inj[:, cols] = (acc[2 * h : 2 * h + 2, :] + net_ref[:, cols].astype(jnp.float32)).astype(jnp.bfloat16)

    pl.semaphore_wait(barrier, len(partners))
    arrive_x, arrive_y = [], []
    for k, (dy, dx) in enumerate(xy_offsets):
        y_, x_ = xy(dy, dx)
        arrive_x.append(send(window_x(inj, x_), recv_in.at[me, :, pl.ds(0, wx)], s_i.at[2 * k], r_i.at[2 * k], at(z, y_, x_)))
    own_ix = pltpu.make_async_copy(window_x(inj, x), recv_in.at[me, :, pl.ds(0, wx)], l_i.at[0])
    own_ix.start()
    for k, (dy, dx) in enumerate(xy_offsets):
        y_, x_ = xy(dy, dx)
        arrive_y.append(send(window_y(inj, y_), recv_in.at[me, :, pl.ds(wx, wy)], s_i.at[2 * k + 1], r_i.at[2 * k + 1], at(z, y_, x_)))
    own_iy = pltpu.make_async_copy(window_y(inj, y), recv_in.at[me, :, pl.ds(wx, wy)], l_i.at[1])
    own_iy.start()
    factor_piece(0)

    cls = cls_ref[...]
    limit = jnp.zeros(cls.shape, jnp.float32)
    price = jnp.zeros(cls.shape, jnp.float32)
    for k in range(classes):
        limit = jnp.where(cls == k, lim_ref[:, k : k + 1], limit)
        price = jnp.where(cls == k, price_ref[:, k : k + 1], price)

    for s in range(2):
        hot[s] = jnp.where(here & (odd == (s == 1)), 1.0, 0.0).astype(jnp.bfloat16)
    flight = {}

    def ring_gather(step, d, c):
        start, size = chunks[c]
        if step > 1:
            flight[step - 1, d, c].wait_recv()
        n = (z + NZ - (step - 1)) % NZ if d == 0 else (z + (step - 1)) % NZ
        block = xall.at[n, :, pl.ds(start, size)]
        flight[step, d, c] = send(block, block, s_z.at[d, step - 1, c], r_z.at[d, step - 1, c], at(zup if d == 0 else zdn, y, x))

    own_ix.wait()
    for c in arrive_x:
        c.wait_recv()
    for i in range(NX * NY):
        xall[z, 2 * i : 2 * i + 2, 0:wx] = recv_in[i, :, 0:wx]
    for d in range(2):
        ring_gather(1, d, 0)
    own_iy.wait()
    for c in arrive_y:
        c.wait_recv()
    for i in range(NX * NY):
        xall[z, 2 * i : 2 * i + 2, wx:width] = recv_in[i, :, wx:width]
    for c in range(1, len(chunks)):
        for d in range(2):
            ring_gather(1, d, c)
    factor_piece(1)
    half = NZ // 2
    for step in range(2, half):
        for c in range(len(chunks)):
            for d in range(2):
                ring_gather(step, d, c)
        if step == 2:
            for p in range(2, PIECES):
                factor_piece(p)
    for c in range(len(chunks)):
        ring_gather(half, way[c], c)
    for c in range(len(chunks)):
        flight[half - 1, 1 - way[c], c].wait_recv()
        flight[half, way[c], c].wait_recv()

    own_px.wait()
    own_py.wait()
    for c in factor:
        c.wait_recv()
    scen = NZ * 2 * NX * NY
    branches = ptdf_ref.shape[0]
    scen = NZ * 2 * NX * NY
    def quarter(d):
        return pl.ds(pl.multiple_of((bus + d) % nbus * part_rows, part_rows), part_rows)

    slots = [(x + k) % NX for k in range(1, NX)] + [NX + yother, x]
    back = []

    def to_holder(j):
        for d in range(nbus):
            if (j, d) != (NX, 0):
                back.append(send(fpart.at[slots[j], quarter(d), :], frecv.at[j, d], s_f.at[j, d], r_f.at[j, d], across(j, d)))

    part = mm(xall[:, :, 0:wx].reshape(scen, wx), px[...].reshape(NX * branches, wx), NT)
    for q in range(NX):
        fpart[q] = part[:, q * branches : (q + 1) * branches]
    for j in range(NX - 1):
        to_holder(j)
    part = mm(xall[:, :, wx:width].reshape(scen, wy), py[...].reshape(NY * branches, wy), NT)
    for q in range(NY):
        fpart[NX + q] = part[:, q * branches : (q + 1) * branches]
    to_holder(NX - 1)
    fpart[x] = fpart[x] + fpart[NX + y]
    to_holder(NX)
    flows = fpart[x, quarter(0), :]
    for c in back:
        c.wait_recv()
    for j in range(NX + 1):
        for d in range(nbus):
            if (j, d) != (NX, 0):
                flows = flows + frecv[j, d]
    upper = jax.nn.sigmoid((flows - limit) / SMOOTH)
    lower = jax.nn.sigmoid((-flows - limit) / SMOOTH)
    gx[x, quarter(0), :] = (price * (upper - lower)).astype(jnp.bfloat16)
    given = {}
    mine = gx.at[x, quarter(0), :]
    for j in (NX, NX - 1, 0, 1, 2):
        there = gy.at[y, quarter(0), :] if j == NX - 1 else mine
        given[j] = [
            send(mine, there, s_g.at[j, d], r_g.at[j, d], across(j, d)) for d in range(nbus) if (j, d) != (NX, 0)
        ]
    for j in (NX, NX - 1):
        for c in given[j]:
            c.wait_recv()
    gy[y] = gx[x]

    def product(g, p, n):
        lhs = jnp.concatenate([g[q] for q in range(n)], axis=1)
        total = mm(lhs, p[...].reshape(n * branches, p.shape[2]), NN)
        return total.reshape(NZ, scen // NZ, p.shape[2])

    down = {}

    def ring_reduce(step, d, c):
        start, size = chunks[c]
        away = half + 1 - step
        target = (z + away) % NZ if d == 0 else (z + NZ - away) % NZ
        value = gpart[target, :, start : start + size]
        if (step - 1, d, c) in down:
            down[step - 1, d, c].wait_recv()
            value = value + ring[1, d, step - 2, :, start : start + size].astype(jnp.float32)
        ring[0, d, step - 1, :, start : start + size] = value.astype(jnp.bfloat16)
        down[step, d, c] = send(
            ring.at[0, d, step - 1, :, pl.ds(start, size)],
            ring.at[1, d, step - 1, :, pl.ds(start, size)],
            s_r.at[d, step - 1, c], r_r.at[d, step - 1, c],
            at(zup if d == 0 else zdn, y, x),
        )

    order = (1, 2, 3, 0)
    gpart[:, :, wx:width] = product(gy, py, NY)
    for c in order:
        if c == 0:
            for j in range(NX - 1):
                for arrived in given[j]:
                    arrived.wait_recv()
            gpart[:, :, 0:wx] = product(gx, px, NX)
        ring_reduce(1, way[c], c)
        ring_reduce(2, 1 - way[c], c)
    for c in order:
        ring_reduce(2, way[c], c)
    for step in range(3, half + 1):
        for c in order:
            ring_reduce(step, 1 - way[c], c)
        for c in order:
            ring_reduce(step, way[c], c)
    last = []
    for c in order:
        start, size = chunks[c]
        value = gpart[z, :, start : start + size]
        for d in range(2):
            down[half, d, c].wait_recv()
            value = value + ring[1, d, half - 1, :, start : start + size].astype(jnp.float32)
        for i in range(NX * NY):
            sbuf[i, :, start : start + size] = value[2 * i : 2 * i + 2, :]
        if c in (3, 0):
            start, size = (0, wx) if c == 0 else (wx, wy)
            for k, (dy, dx) in enumerate(xy_offsets):
                y2, x2 = xy(dy, dx)
                last.append(send(
                    sbuf.at[y2 * NX + x2, :, pl.ds(start, size)], srecv.at[me, :, pl.ds(start, size)],
                    s_s.at[k, c % 2], r_s.at[k, c % 2], at(z, y2, x2),
                ))
    srecv[me] = sbuf[me]

    def pick(first, count):
        for h in range(first, first + count):
            rows[2 * h : 2 * h + 2, :] = gbus_ref[:, h * LANES : (h + 1) * LANES]
        parts = jnp.concatenate(split3(rows[2 * first : 2 * (first + count), :]), axis=1)
        both = []
        for s in range(2):
            picked = mm(parts, hot[s, 2 * first : 2 * (first + count), :], TN)
            both.append(picked[0:LANES] + picked[LANES : 2 * LANES] + picked[2 * LANES :])
        return both

    for c in last[: NX * NY - 1]:
        c.wait_recv()
    for q in range(NY):
        part = srecv[q * NX, :, wx:width]
        for j in range(1, NX):
            part = part + srecv[q * NX + j, :, wx:width]
        gbus_ref[:, base_y + q * wy : base_y + (q + 1) * wy] = part
    picked_y = pick(NX * tx, NY * ty)
    for c in last[NX * NY - 1 :]:
        c.wait_recv()
    for q in range(NX):
        part = srecv[q, :, 0:wx]
        for j in range(1, NY):
            part = part + srecv[j * NX + q, :, 0:wx]
        gbus_ref[:, q * wx : (q + 1) * wx] = part
    picked_x = pick(0, NX * tx)
    lo_mask = lo_id == lo
    for s in range(2):
        picked = jnp.sum(jnp.where(lo_mask, picked_x[s] + picked_y[s], 0.0), axis=0, keepdims=True)
        prel[bus, s : s + 1, :] = picked * eff
    release = []
    for d in range(1, nbus):
        release.append(send(prel.at[bus], prel.at[bus], s_o.at[d - 1], r_o.at[d - 1], (br, (bus + d) % nbus)))
    for c in release:
        c.wait_recv()
    out = prel[0]
    for b in range(1, nbus):
        out = out + prel[b]
    grel_ref[...] = out
    for c in sends:
        c.wait_send()


def finish(gbus_in, grel_in, gbus_ref, grel_ref):
    gbus_ref[...] = gbus_in[...]
    grel_ref[...] = grel_in[...]


def shards(net_load, release, plant_bus, efficiency, ptdf, branch_class, class_limit, class_price):
    nbus = 4
    plants = plant_bus.shape[0]
    classes = class_limit.shape[0]
    branches, columns = ptdf.shape
    tiles = columns // LANES
    tx = 15
    ty = (tiles - NX * tx) // NY
    wx, wy = tx * LANES, ty * LANES
    width = wx + wy
    group = NX * NY
    scen = NZ * group * 2
    bf, f32 = jnp.bfloat16, jnp.float32
    dma = pltpu.SemaphoreType.DMA
    vmem = pl.BlockSpec(memory_space=pltpu.VMEM)
    out = pl.pallas_call(
        functools.partial(kernel, (tiles, tx, ty, nbus, plants, classes)),
        out_shape=(
            jax.ShapeDtypeStruct((2, columns), f32),
            jax.ShapeDtypeStruct((2, plants), f32),
        ),
        in_specs=[pl.BlockSpec(memory_space=pl.ANY)] * 8,
        out_specs=(vmem, vmem),
        scratch_shapes=[
            pltpu.VMEM((2, columns), bf),
            pltpu.VMEM((2, plants), f32),
            pltpu.VMEM((1, plants), jnp.int32),
            pltpu.VMEM((1, plants), f32),
            pltpu.VMEM((1, branches), jnp.int32),
            pltpu.VMEM((1, classes), f32),
            pltpu.VMEM((1, classes), f32),
            pltpu.VMEM((2, columns), bf),
            pltpu.VMEM((2 * tiles, LANES), f32),
            pltpu.VMEM((NX, branches, wx), bf),
            pltpu.VMEM((NY, branches, wy), bf),
            pltpu.VMEM((group, 2, width), bf),
            pltpu.VMEM((NZ, 2 * group, width), bf),
            pltpu.VMEM((NX + NY, scen, branches), f32),
            pltpu.VMEM((NX + 1, nbus, scen // nbus, branches), f32),
            pltpu.VMEM((NX, scen, branches), bf),
            pltpu.VMEM((NY, scen, branches), bf),
            pltpu.VMEM((NZ, 2 * group, width), f32),
            pltpu.VMEM((2, 2, NZ // 2, 2 * group, width), bf),
            pltpu.VMEM((group, 2, width), f32),
            pltpu.VMEM((group, 2, width), f32),
            pltpu.VMEM((2 * tiles, LANES), f32),
            pltpu.VMEM((nbus, 2, plants), f32),
            pltpu.VMEM((2, 2 * tiles, plants), bf),
            dma((7,)), dma((NX, PIECES)), dma((NX, PIECES)), dma((2,)),
            dma((2 * (group - 1),)), dma((2 * (group - 1),)), dma((2,)),
            dma((2, NZ // 2, 4)), dma((2, NZ // 2, 4)),
            dma((NX + 1, nbus)), dma((NX + 1, nbus)),
            dma((NX + 1, nbus)), dma((NX + 1, nbus)),
            dma((2, NZ // 2, 4)), dma((2, NZ // 2, 4)),
            dma((group - 1, 2)), dma((group - 1, 2)),
            dma((nbus - 1,)), dma((nbus - 1,)),
        ],
        compiler_params=pltpu.CompilerParams(
            collective_id=0, has_side_effects=True, vmem_limit_bytes=56 << 20
        ),
    )(
        net_load,
        release,
        plant_bus[None, :],
        efficiency[None, :],
        ptdf,
        branch_class[None, :],
        class_limit[None, :],
        class_price[None, :],
    )
    return pl.pallas_call(
        finish,
        out_shape=(jax.ShapeDtypeStruct((2, columns), f32), jax.ShapeDtypeStruct((2, plants), f32)),
        in_specs=[vmem] * 2,
        out_specs=(vmem, vmem),
    )(*out)


def solution(mesh):
    placed = (P("br", "bus"), P("br", None), P(), P(), P("br", "bus"), P("br"), P(), P())
    return jax.shard_map(
        shards,
        mesh=mesh,
        in_specs=placed,
        out_specs=(P("br", "bus"), P("br", None)),
        check_vma=False,
    )
```

```python
import functools

import jax
import jax.numpy as jnp
from jax import lax
from jax.experimental import pallas as pl
from jax.experimental.pallas import tpu as pltpu
from jax.sharding import PartitionSpec as P

SMOOTH = 0.25
LANES = 128
NX, NY, NZ = 4, 2, 8
PIECES = 4
MESH = pl.DeviceIdType.MESH
NT = (((1,), (1,)), ((), ()))
TN = (((0,), (0,)), ((), ()))
NN = (((1,), (0,)), ((), ()))


def mm(a, b, dims):
    return lax.dot_general(a, b, dims, preferred_element_type=jnp.float32)


def split3(v):
    one = v.astype(jnp.bfloat16)
    rest = v - one.astype(jnp.float32)
    two = rest.astype(jnp.bfloat16)
    three = (rest - two.astype(jnp.float32)).astype(jnp.bfloat16)
    return one, two, three


def kernel(
    sizes,
    net_in, rel_in, plant_in, eff_in, ptdf_ref, cls_in, lim_in, price_in,
    gbus_ref, grel_ref,
    net_ref, rel_ref, plant_ref, eff_ref, cls_ref, lim_ref, price_ref,
    inj, acc, px, py, recv_in, xall, fpart, frecv, gx, gy, gpart, ring, sbuf, srecv, rows, prel, hot,
    l_in, s_p, r_p, l_p, s_i, r_i, l_i, s_z, r_z, s_f, r_f, s_g, r_g, s_r, r_r, s_s, r_s, s_o, r_o,
):
    tiles, tx, ty, nbus, plants, classes = sizes
    wx, wy = tx * LANES, ty * LANES
    base_y = NX * wx
    width = wx + wy
    part_rows = 2 * NZ * NX * NY // nbus
    third = (ty + 2) // 3 * LANES
    chunks = ((0, wx), (wx, third), (wx + third, third), (wx + 2 * third, wy - 2 * third))
    way = (1, 0, 0, 1)
    br, bus = lax.axis_index("br"), lax.axis_index("bus")
    z, y, x = br // (NX * NY), (br // NX) % NY, br % NX
    me = y * NX + x

    def at(z_, y_, x_):
        return ((z_ * NY + y_) * NX + x_, bus)

    xy_offsets = [(dy, dx) for dy in range(NY) for dx in range(NX) if (dy, dx) != (0, 0)]

    def xy(dy, dx):
        return (y + dy) % NY, (x + dx) % NX

    zup, zdn = (z + 1) % NZ, (z + NZ - 1) % NZ
    partners = [at(z, *xy(dy, dx)) for dy, dx in xy_offsets]
    partners += [at(zup, y, x), at(zdn, y, x)]
    partners += [(br, (bus + d) % nbus) for d in range(1, nbus)]
    yother = (y + 1) % NY
    holders = [(z, y, (x + k) % NX) for k in range(1, NX)] + [(z, yother, x), (z, y, x)]

    def across(j, d):
        z_, y_, x_ = holders[j]
        return ((z_ * NY + y_) * NX + x_, (bus + d) % nbus)

    partners += [across(j, d) for j in range(NX) for d in range(1, nbus)]

    barrier = pltpu.get_barrier_semaphore()
    for p in partners:
        pl.semaphore_signal(barrier, inc=1, device_id=p, device_id_type=MESH)

    loads = [
        pltpu.make_async_copy(src, dst, l_in.at[i])
        for i, (src, dst) in enumerate((
            (plant_in, plant_ref), (rel_in, rel_ref), (eff_in, eff_ref), (net_in, net_ref),
            (cls_in, cls_ref), (lim_in, lim_ref), (price_in, price_ref),
        ))
    ]
    for c in loads:
        c.start()

    sends = []

    def send(src, dst, ss, rs, dev):
        c = pltpu.make_async_remote_copy(
            src_ref=src, dst_ref=dst, send_sem=ss, recv_sem=rs, device_id=dev, device_id_type=MESH
        )
        c.start()
        sends.append(c)
        return c

    def window_x(ref, q):
        return ref.at[:, pl.ds(pl.multiple_of(q * wx, LANES), wx)]

    def window_y(ref, q):
        return ref.at[:, pl.ds(pl.multiple_of(base_y + q * wy, LANES), wy)]

    own_px = pltpu.make_async_copy(window_x(ptdf_ref, x), px.at[x], l_p.at[0])
    own_py = pltpu.make_async_copy(window_y(ptdf_ref, y), py.at[y], l_p.at[1])
    own_px.start()
    own_py.start()

    for c in loads:
        c.wait()
    factor = []
    piece = ptdf_ref.shape[0] // PIECES

    def factor_piece(p):
        r = pl.ds(p * piece, piece)
        for k in (2, 1, 3):
            x_ = (x + k) % NX
            factor.append(send(
                ptdf_ref.at[r, pl.ds(pl.multiple_of(x_ * wx, LANES), wx)], px.at[x, r, :],
                s_p.at[k - 1, p], r_p.at[k - 1, p], at(z, y, x_),
            ))
        factor.append(send(
            ptdf_ref.at[r, pl.ds(pl.multiple_of(base_y + yother * wy, LANES), wy)], py.at[y, r, :],
            s_p.at[NX - 1, p], r_p.at[NX - 1, p], at(z, yother, x),
        ))

    col = plant_ref[...] - bus * (tiles * LANES)
    hi = col >> 7
    lo = col & 127
    row_id = lax.broadcasted_iota(jnp.int32, (2 * tiles, plants), 0)
    lo_id = lax.broadcasted_iota(jnp.int32, (LANES, plants), 0)
    lo_hot = (lo_id == lo).astype(jnp.float32).astype(jnp.bfloat16)
    eff = eff_ref[...]
    weight = rel_ref[...] * eff
    here = (row_id >> 1) == hi
    odd = (row_id & 1) == 1
    total = None
    for part in split3(weight):
        part = part.astype(jnp.float32)
        placed = jnp.where(here, jnp.where(odd, part[1:2, :], part[0:1, :]), 0.0)
        term = mm(placed.astype(jnp.bfloat16), lo_hot, NT)
        total = term if total is None else total + term
    acc[...] = total
    for h in range(tiles):
        cols = slice(h * LANES, (h + 1) * LANES)
        inj[:, cols] = (acc[2 * h : 2 * h + 2, :] + net_ref[:, cols].astype(jnp.float32)).astype(jnp.bfloat16)

    pl.semaphore_wait(barrier, len(partners))
    arrive_x, arrive_y = [], []
    for k, (dy, dx) in enumerate(xy_offsets):
        y_, x_ = xy(dy, dx)
        arrive_x.append(send(window_x(inj, x_), recv_in.at[me, :, pl.ds(0, wx)], s_i.at[2 * k], r_i.at[2 * k], at(z, y_, x_)))
    own_ix = pltpu.make_async_copy(window_x(inj, x), recv_in.at[me, :, pl.ds(0, wx)], l_i.at[0])
    own_ix.start()
    for k, (dy, dx) in enumerate(xy_offsets):
        y_, x_ = xy(dy, dx)
        arrive_y.append(send(window_y(inj, y_), recv_in.at[me, :, pl.ds(wx, wy)], s_i.at[2 * k + 1], r_i.at[2 * k + 1], at(z, y_, x_)))
    own_iy = pltpu.make_async_copy(window_y(inj, y), recv_in.at[me, :, pl.ds(wx, wy)], l_i.at[1])
    own_iy.start()
    factor_piece(0)

    cls = cls_ref[...]
    limit = jnp.zeros(cls.shape, jnp.float32)
    price = jnp.zeros(cls.shape, jnp.float32)
    for k in range(classes):
        limit = jnp.where(cls == k, lim_ref[:, k : k + 1], limit)
        price = jnp.where(cls == k, price_ref[:, k : k + 1], price)

    for s in range(2):
        hot[s] = jnp.where(here & (odd == (s == 1)), 1.0, 0.0).astype(jnp.bfloat16)
    flight = {}

    def ring_gather(step, d, c):
        start, size = chunks[c]
        if step > 1:
            flight[step - 1, d, c].wait_recv()
        n = (z + NZ - (step - 1)) % NZ if d == 0 else (z + (step - 1)) % NZ
        block = xall.at[n, :, pl.ds(start, size)]
        flight[step, d, c] = send(block, block, s_z.at[d, step - 1, c], r_z.at[d, step - 1, c], at(zup if d == 0 else zdn, y, x))

    own_ix.wait()
    for c in arrive_x:
        c.wait_recv()
    for i in range(NX * NY):
        xall[z, 2 * i : 2 * i + 2, 0:wx] = recv_in[i, :, 0:wx]
    for d in range(2):
        ring_gather(1, d, 0)
    own_iy.wait()
    for c in arrive_y:
        c.wait_recv()
    for i in range(NX * NY):
        xall[z, 2 * i : 2 * i + 2, wx:width] = recv_in[i, :, wx:width]
    for c in range(1, len(chunks)):
        for d in range(2):
            ring_gather(1, d, c)
    factor_piece(1)
    half = NZ // 2
    for step in range(2, half):
        for c in range(len(chunks)):
            for d in range(2):
                ring_gather(step, d, c)
        if step == 2:
            for p in range(2, PIECES):
                factor_piece(p)
    for c in range(len(chunks)):
        ring_gather(half, way[c], c)
    for c in range(len(chunks)):
        flight[half - 1, 1 - way[c], c].wait_recv()
        flight[half, way[c], c].wait_recv()

    own_px.wait()
    own_py.wait()
    for c in factor:
        c.wait_recv()
    scen = NZ * 2 * NX * NY
    branches = ptdf_ref.shape[0]
    scen = NZ * 2 * NX * NY
    def quarter(d):
        return pl.ds(pl.multiple_of((bus + d) % nbus * part_rows, part_rows), part_rows)

    slots = [(x + k) % NX for k in range(1, NX)] + [NX + yother, x]
    back = []

    def to_holder(j):
        for d in range(nbus):
            if (j, d) != (NX, 0):
                back.append(send(fpart.at[slots[j], quarter(d), :], frecv.at[j, d], s_f.at[j, d], r_f.at[j, d], across(j, d)))

    part = mm(xall[:, :, 0:wx].reshape(scen, wx), px[...].reshape(NX * branches, wx), NT)
    for q in range(NX):
        fpart[q] = part[:, q * branches : (q + 1) * branches]
    for j in range(NX - 1):
        to_holder(j)
    part = mm(xall[:, :, wx:width].reshape(scen, wy), py[...].reshape(NY * branches, wy), NT)
    for q in range(NY):
        fpart[NX + q] = part[:, q * branches : (q + 1) * branches]
    to_holder(NX - 1)
    fpart[x] = fpart[x] + fpart[NX + y]
    to_holder(NX)
    flows = fpart[x, quarter(0), :]
    for c in back:
        c.wait_recv()
    for j in range(NX + 1):
        for d in range(nbus):
            if (j, d) != (NX, 0):
                flows = flows + frecv[j, d]
    upper = jax.nn.sigmoid((flows - limit) / SMOOTH)
    lower = jax.nn.sigmoid((-flows - limit) / SMOOTH)
    gx[x, quarter(0), :] = (price * (upper - lower)).astype(jnp.bfloat16)
    given = {}
    mine = gx.at[x, quarter(0), :]
    for j in (NX - 1, 1, 0, 2, NX):
        there = gy.at[y, quarter(0), :] if j == NX - 1 else mine
        given[j] = [
            send(mine, there, s_g.at[j, d], r_g.at[j, d], across(j, d)) for d in range(nbus) if (j, d) != (NX, 0)
        ]
    for j in (NX, NX - 1):
        for c in given[j]:
            c.wait_recv()
    gy[y] = gx[x]

    def product(g, p, n):
        lhs = jnp.concatenate([g[q] for q in range(n)], axis=1)
        total = mm(lhs, p[...].reshape(n * branches, p.shape[2]), NN)
        return total.reshape(NZ, scen // NZ, p.shape[2])

    down = {}

    def ring_reduce(step, d, c):
        start, size = chunks[c]
        away = half + 1 - step
        target = (z + away) % NZ if d == 0 else (z + NZ - away) % NZ
        value = gpart[target, :, start : start + size]
        if (step - 1, d, c) in down:
            down[step - 1, d, c].wait_recv()
            value = value + ring[1, d, step - 2, :, start : start + size].astype(jnp.float32)
        ring[0, d, step - 1, :, start : start + size] = value.astype(jnp.bfloat16)
        down[step, d, c] = send(
            ring.at[0, d, step - 1, :, pl.ds(start, size)],
            ring.at[1, d, step - 1, :, pl.ds(start, size)],
            s_r.at[d, step - 1, c], r_r.at[d, step - 1, c],
            at(zup if d == 0 else zdn, y, x),
        )

    order = (1, 2, 3, 0)
    gpart[:, :, wx:width] = product(gy, py, NY)
    for c in order:
        if c == 0:
            for j in range(NX - 1):
                for arrived in given[j]:
                    arrived.wait_recv()
            gpart[:, :, 0:wx] = product(gx, px, NX)
        ring_reduce(1, way[c], c)
        ring_reduce(2, 1 - way[c], c)
    for c in order:
        ring_reduce(2, way[c], c)
    for step in range(3, half + 1):
        for c in order:
            ring_reduce(step, 1 - way[c], c)
        for c in order:
            ring_reduce(step, way[c], c)
    last = []
    for c in order:
        start, size = chunks[c]
        value = gpart[z, :, start : start + size]
        for d in range(2):
            down[half, d, c].wait_recv()
            value = value + ring[1, d, half - 1, :, start : start + size].astype(jnp.float32)
        for i in range(NX * NY):
            sbuf[i, :, start : start + size] = value[2 * i : 2 * i + 2, :]
        if c in (3, 0):
            start, size = (0, wx) if c == 0 else (wx, wy)
            for k, (dy, dx) in enumerate(xy_offsets):
                y2, x2 = xy(dy, dx)
                last.append(send(
                    sbuf.at[y2 * NX + x2, :, pl.ds(start, size)], srecv.at[me, :, pl.ds(start, size)],
                    s_s.at[k, c % 2], r_s.at[k, c % 2], at(z, y2, x2),
                ))
    srecv[me] = sbuf[me]

    def pick(first, count):
        for h in range(first, first + count):
            rows[2 * h : 2 * h + 2, :] = gbus_ref[:, h * LANES : (h + 1) * LANES]
        parts = jnp.concatenate(split3(rows[2 * first : 2 * (first + count), :]), axis=1)
        both = []
        for s in range(2):
            picked = mm(parts, hot[s, 2 * first : 2 * (first + count), :], TN)
            both.append(picked[0:LANES] + picked[LANES : 2 * LANES] + picked[2 * LANES :])
        return both

    for c in last[: NX * NY - 1]:
        c.wait_recv()
    for q in range(NY):
        part = srecv[q * NX, :, wx:width]
        for j in range(1, NX):
            part = part + srecv[q * NX + j, :, wx:width]
        gbus_ref[:, base_y + q * wy : base_y + (q + 1) * wy] = part
    picked_y = pick(NX * tx, NY * ty)
    for c in last[NX * NY - 1 :]:
        c.wait_recv()
    for q in range(NX):
        part = srecv[q, :, 0:wx]
        for j in range(1, NY):
            part = part + srecv[j * NX + q, :, 0:wx]
        gbus_ref[:, q * wx : (q + 1) * wx] = part
    picked_x = pick(0, NX * tx)
    lo_mask = lo_id == lo
    for s in range(2):
        picked = jnp.sum(jnp.where(lo_mask, picked_x[s] + picked_y[s], 0.0), axis=0, keepdims=True)
        prel[bus, s : s + 1, :] = picked * eff
    release = []
    for d in range(1, nbus):
        release.append(send(prel.at[bus], prel.at[bus], s_o.at[d - 1], r_o.at[d - 1], (br, (bus + d) % nbus)))
    for c in release:
        c.wait_recv()
    out = prel[0]
    for b in range(1, nbus):
        out = out + prel[b]
    grel_ref[...] = out
    for c in sends:
        c.wait_send()


def finish(gbus_in, grel_in, gbus_ref, grel_ref):
    gbus_ref[...] = gbus_in[...]
    grel_ref[...] = grel_in[...]


def shards(net_load, release, plant_bus, efficiency, ptdf, branch_class, class_limit, class_price):
    nbus = 4
    plants = plant_bus.shape[0]
    classes = class_limit.shape[0]
    branches, columns = ptdf.shape
    tiles = columns // LANES
    tx = 15
    ty = (tiles - NX * tx) // NY
    wx, wy = tx * LANES, ty * LANES
    width = wx + wy
    group = NX * NY
    scen = NZ * group * 2
    bf, f32 = jnp.bfloat16, jnp.float32
    dma = pltpu.SemaphoreType.DMA
    vmem = pl.BlockSpec(memory_space=pltpu.VMEM)
    out = pl.pallas_call(
        functools.partial(kernel, (tiles, tx, ty, nbus, plants, classes)),
        out_shape=(
            jax.ShapeDtypeStruct((2, columns), f32),
            jax.ShapeDtypeStruct((2, plants), f32),
        ),
        in_specs=[pl.BlockSpec(memory_space=pl.ANY)] * 8,
        out_specs=(vmem, vmem),
        scratch_shapes=[
            pltpu.VMEM((2, columns), bf),
            pltpu.VMEM((2, plants), f32),
            pltpu.VMEM((1, plants), jnp.int32),
            pltpu.VMEM((1, plants), f32),
            pltpu.VMEM((1, branches), jnp.int32),
            pltpu.VMEM((1, classes), f32),
            pltpu.VMEM((1, classes), f32),
            pltpu.VMEM((2, columns), bf),
            pltpu.VMEM((2 * tiles, LANES), f32),
            pltpu.VMEM((NX, branches, wx), bf),
            pltpu.VMEM((NY, branches, wy), bf),
            pltpu.VMEM((group, 2, width), bf),
            pltpu.VMEM((NZ, 2 * group, width), bf),
            pltpu.VMEM((NX + NY, scen, branches), f32),
            pltpu.VMEM((NX + 1, nbus, scen // nbus, branches), f32),
            pltpu.VMEM((NX, scen, branches), bf),
            pltpu.VMEM((NY, scen, branches), bf),
            pltpu.VMEM((NZ, 2 * group, width), f32),
            pltpu.VMEM((2, 2, NZ // 2, 2 * group, width), bf),
            pltpu.VMEM((group, 2, width), f32),
            pltpu.VMEM((group, 2, width), f32),
            pltpu.VMEM((2 * tiles, LANES), f32),
            pltpu.VMEM((nbus, 2, plants), f32),
            pltpu.VMEM((2, 2 * tiles, plants), bf),
            dma((7,)), dma((NX, PIECES)), dma((NX, PIECES)), dma((2,)),
            dma((2 * (group - 1),)), dma((2 * (group - 1),)), dma((2,)),
            dma((2, NZ // 2, 4)), dma((2, NZ // 2, 4)),
            dma((NX + 1, nbus)), dma((NX + 1, nbus)),
            dma((NX + 1, nbus)), dma((NX + 1, nbus)),
            dma((2, NZ // 2, 4)), dma((2, NZ // 2, 4)),
            dma((group - 1, 2)), dma((group - 1, 2)),
            dma((nbus - 1,)), dma((nbus - 1,)),
        ],
        compiler_params=pltpu.CompilerParams(
            collective_id=0, has_side_effects=True, vmem_limit_bytes=56 << 20
        ),
    )(
        net_load,
        release,
        plant_bus[None, :],
        efficiency[None, :],
        ptdf,
        branch_class[None, :],
        class_limit[None, :],
        class_price[None, :],
    )
    return pl.pallas_call(
        finish,
        out_shape=(jax.ShapeDtypeStruct((2, columns), f32), jax.ShapeDtypeStruct((2, plants), f32)),
        in_specs=[vmem] * 2,
        out_specs=(vmem, vmem),
    )(*out)


def solution(mesh):
    placed = (P("br", "bus"), P("br", None), P(), P(), P("br", "bus"), P("br"), P(), P())
    return jax.shard_map(
        shards,
        mesh=mesh,
        in_specs=placed,
        out_specs=(P("br", "bus"), P("br", None)),
        check_vma=False,
    )
```
